32 devices in a mesh: depth: 8 (over z, core), freq: 4 (over y, x).
Axes of the slice: x: 2, y: 2, z: 4, core: 2. Of those that a mesh axis runs over, the one named last changes fastest.
Arguments:
- fields_top: bfloat16 [8, 2, 4, 2, 384, 384], P('depth', None, 'freq'), may hold values from -6 to 6
- surface: bfloat16 [2, 2, 4, 2, 384, 384], P(None, None, 'freq'), may hold values from -6 to 6
- up_state: bfloat16 [8, 4, 2, 384, 384], P('depth', 'freq'), may hold values from -6 to 6
- angular_freq: float32 [4], P('freq'), may hold values from 0.5 to 2.5
- class_slowness: float32 [8], replicated, may hold values from 0.6 to 1.3
- velocity_class: int32 [8, 12, 12], P('depth'), may hold values from 0 to 7
- slowness_detail: float32 [8, 384, 384], P('depth'), may hold values from 0.5 to 1.5
Outputs:
- reflectivity: bfloat16 [8, 384, 384], P('depth', 'freq')
- up_out: bfloat16 [8, 4, 2, 384, 384], P('depth', 'freq')
The draws below stay inside these ranges and needn't reach their ends.
All inputs are finite; a program needn't handle non-finite values.
Results may differ from the reference program's by a relative error of at most 0.023.
Values may be sent and summed in bfloat16 or wider, within the bound.
A program may use at most 64 MiB of HBM per device.

```python
import math
import jax
import jax.numpy as jnp
from jax import lax

N = 384
LAYERS = 1
TICKS = 3
CLASSES = 8
BLOCK = 32
FREQS = 4
SECTIONS = 8
DEPTH_LAYERS = 8


def touch_ends(array, own_key, smallest, high):
    longest = array.shape.index(max(array.shape))
    spots = []
    for shift in (0, 1):
        where = [jax.random.randint(jax.random.fold_in(own_key, axis), (), 0, length) for axis, length in enumerate(array.shape)]
        where[longest] = (where[longest] + shift) % array.shape[longest]
        spots.append(tuple(where))
    return array.at[spots[0]].set(smallest).at[spots[1]].set(high)


def shard_levels(own_key, dims, cuts, low, largest):
    def one(dim, parts):
        steps = jax.random.uniform(jax.random.fold_in(jax.random.fold_in(own_key, 6), dim), (parts,), jnp.float32, low / len(cuts), largest / len(cuts))
        return jnp.repeat(jnp.exp(steps), dims[dim] // parts).reshape((-1,) + (1,) * (len(dims) - dim - 1))

    gain = one(*cuts[0])
    for cut in cuts[1:]:
        gain = gain * one(*cut)
    return gain


def bell_draw(own_key, shape, scale, limit, cuts=(), held_as=jnp.bfloat16):
    gain = shard_levels(own_key, shape, cuts, -0.22, 0.18) if cuts else 1.0
    drawn = jax.random.normal(own_key, shape, jnp.float32) * scale * gain
    return jnp.minimum(jnp.maximum(drawn, -limit), limit).astype(held_as)


def setup_inputs(seed: int = 0) -> dict:
    arg_keys = jax.random.split(jax.random.key(seed), 8)
    fields_top = bell_draw(arg_keys[0], (SECTIONS, 2, FREQS, 2, N, N), 1.0, 6.0, ((0, 8), (2, 4)))
    surface = bell_draw(arg_keys[1], (TICKS - 1, 2, FREQS, 2, N, N), 1.0, 6.0, ((2, 4),))
    up_state = bell_draw(arg_keys[2], (SECTIONS, FREQS, 2, N, N), 1.0, 6.0, ((0, 8), (1, 4)))
    angular_freq = jnp.clip(0.5 + 2.0 * jax.random.uniform(arg_keys[3], (FREQS,), jnp.float32) ** shard_levels(arg_keys[3], (FREQS,), ((0, 4),), -0.2, 0.2), 0.5, 2.5)
    class_slowness = jnp.clip(jnp.exp(jax.random.uniform(arg_keys[4], (CLASSES,), jnp.float32, math.log(0.6), math.log(1.3))), 0.6, 1.3)
    velocity_class = touch_ends(jax.random.randint(arg_keys[5], (DEPTH_LAYERS, N // BLOCK, N // BLOCK), 0, CLASSES), jax.random.fold_in(arg_keys[5], 1), 0, CLASSES - 1).astype(jnp.int32)
    slowness_detail = jnp.clip(1.0 + 0.1 * jax.random.normal(arg_keys[6], (DEPTH_LAYERS, N, N), jnp.float32), 0.5, 1.5)
    return {"fields_top": fields_top, "surface": surface, "up_state": up_state, "angular_freq": angular_freq, "class_slowness": class_slowness, "velocity_class": velocity_class, "slowness_detail": slowness_detail}


DEPTH_STEP = 1.0
EPSILON = 1e-06

def make_tables(lateral):
    positions = jnp.arange(lateral, dtype=jnp.int32)
    wrapped = positions[:, None] * positions[None, :] % lateral
    angles = wrapped.astype(jnp.float32) * (2.0 * jnp.pi / lateral)
    cosine_table = jnp.cos(angles).astype(jnp.bfloat16)
    sine_table = jnp.sin(angles).astype(jnp.bfloat16)
    folded = jnp.where(positions < lateral // 2, positions, positions - lateral)
    kappa = folded.astype(jnp.float32) * (2.0 * jnp.pi / lateral)
    wavenumber_sq = kappa[:, None] ** 2 + kappa[None, :] ** 2
    return (cosine_table, sine_table, wavenumber_sq)

def cell_slowness(velocity_class, class_slowness, slowness_detail):
    count, lateral = (slowness_detail.shape[0], slowness_detail.shape[1])
    blocks = lateral // BLOCK
    onehot = (velocity_class[..., None] == jnp.arange(CLASSES, dtype=jnp.int32)).astype(jnp.float32)
    block_slow = lax.optimization_barrier(jnp.sum(onehot * class_slowness, axis=-1))
    spread = jnp.broadcast_to(block_slow[:, :, None, :, None], (count, blocks, BLOCK, blocks, BLOCK))
    slowness = spread.reshape(count, lateral, lateral) * slowness_detail
    return (slowness, lax.optimization_barrier(jnp.mean(slowness, axis=(1, 2))))

def propagate(real_part, imag_part, angular, slowness, reference_slow, cosine_table, sine_table, wavenumber_sq):
    lateral = real_part.shape[0]
    joined_cols = jnp.concatenate([cosine_table, sine_table], axis=1)
    joined_rows = jnp.concatenate([cosine_table, sine_table], axis=0)
    product = jnp.dot(jnp.concatenate([real_part, imag_part], axis=0), joined_cols, preferred_element_type=jnp.float32)
    real_cos, real_sin = (product[:lateral, :lateral], product[:lateral, lateral:])
    imag_cos, imag_sin = (product[lateral:, :lateral], product[lateral:, lateral:])
    half_real = (real_cos + imag_sin).astype(jnp.bfloat16)
    half_imag = (imag_cos - real_sin).astype(jnp.bfloat16)
    product = jnp.dot(joined_rows, jnp.concatenate([half_real, half_imag], axis=1), preferred_element_type=jnp.float32)
    cos_real, cos_imag = (product[:lateral, :lateral], product[:lateral, lateral:])
    sin_real, sin_imag = (product[lateral:, :lateral], product[lateral:, lateral:])
    spec_real = cos_real + sin_imag
    spec_imag = cos_imag - sin_real
    vertical = (angular * reference_slow) ** 2 - wavenumber_sq
    travel = jnp.sqrt(jnp.maximum(vertical, 0.0)) * DEPTH_STEP
    decay = jnp.exp(-jnp.sqrt(jnp.maximum(-vertical, 0.0)) * DEPTH_STEP) / (lateral * lateral)
    phase_real = decay * jnp.cos(travel)
    phase_imag = decay * jnp.sin(travel)
    shifted_real = (spec_real * phase_real - spec_imag * phase_imag).astype(jnp.bfloat16)
    shifted_imag = (spec_real * phase_imag + spec_imag * phase_real).astype(jnp.bfloat16)
    product = jnp.dot(joined_rows, jnp.concatenate([shifted_real, shifted_imag], axis=1), preferred_element_type=jnp.float32)
    cos_real, cos_imag = (product[:lateral, :lateral], product[:lateral, lateral:])
    sin_real, sin_imag = (product[lateral:, :lateral], product[lateral:, lateral:])
    back_real = (cos_real - sin_imag).astype(jnp.bfloat16)
    back_imag = (cos_imag + sin_real).astype(jnp.bfloat16)
    product = jnp.dot(jnp.concatenate([back_real, back_imag], axis=0), joined_cols, preferred_element_type=jnp.float32)
    real_cos, real_sin = (product[:lateral, :lateral], product[:lateral, lateral:])
    imag_cos, imag_sin = (product[lateral:, :lateral], product[lateral:, lateral:])
    space_real = real_cos - imag_sin
    space_imag = imag_cos + real_sin
    lens = angular * DEPTH_STEP * (slowness - reference_slow)
    lens_cos, lens_sin = (jnp.cos(lens), jnp.sin(lens))
    new_real = (space_real * lens_cos - space_imag * lens_sin).astype(jnp.bfloat16)
    new_imag = (space_real * lens_sin + space_imag * lens_cos).astype(jnp.bfloat16)
    return (new_real, new_imag)

def advance(fields, angular, slowness, reference_slow, tables):
    cosine_table, sine_table, wavenumber_sq = tables

    def single(real_part, imag_part, frequency):
        return propagate(real_part, imag_part, frequency, slowness, reference_slow, cosine_table, sine_table, wavenumber_sq)
    new_real, new_imag = jax.vmap(single)(fields[:, 0], fields[:, 1], angular)
    return jnp.stack([new_real, new_imag], axis=1)

def advance_pair(fields, angular, slowness, reference_slow, tables):

    def one_field(member):
        return advance(member, angular, slowness, reference_slow, tables)
    return jax.vmap(one_field)(fields)

def image_terms(fields):
    source = fields[0].astype(jnp.float32)
    receiver = fields[1].astype(jnp.float32)
    image_part = lax.optimization_barrier(jnp.sum(source[:, 0] * receiver[:, 0] + source[:, 1] * receiver[:, 1], axis=0))
    illum_part = lax.optimization_barrier(jnp.sum(source[:, 0] * source[:, 0] + source[:, 1] * source[:, 1], axis=0))
    return (image_part, illum_part)

def reference(fields_top, surface, up_state, angular_freq, class_slowness, velocity_class, slowness_detail):
    lateral = fields_top.shape[-1]
    sections = fields_top.shape[0]
    tables = make_tables(lateral)
    slowness, reference_slow = cell_slowness(velocity_class, class_slowness, slowness_detail)
    total_layers = slowness.shape[0]
    image_sum = [jnp.zeros((lateral, lateral), jnp.float32) for layer_index in range(total_layers)]
    illumination = [jnp.zeros((lateral, lateral), jnp.float32) for layer_index in range(total_layers)]
    sources = [None] * total_layers
    current = [fields_top[section] for section in range(sections)]
    for turn_index in range(TICKS):
        ended = []
        for section in range(sections):
            fields = current[section]
            for inner in range(LAYERS):
                layer_index = section * LAYERS + inner
                fields = advance_pair(fields, angular_freq, slowness[layer_index], reference_slow[layer_index], tables)
                image_part, illum_part = image_terms(fields)
                image_sum[layer_index] = image_sum[layer_index] + image_part
                illumination[layer_index] = illumination[layer_index] + illum_part
                if turn_index == TICKS - 1:
                    sources[layer_index] = fields[0]
            ended.append(fields)
        if turn_index + 1 < TICKS:
            current = [surface[turn_index]] + ended[:-1]
    image_all = jnp.stack(image_sum)
    illum_all = jnp.stack(illumination)
    damping = lax.optimization_barrier(jnp.mean(illum_all, axis=(1, 2)))
    balanced = image_all / (illum_all + damping[:, None, None])
    mean_square = lax.optimization_barrier(jnp.mean(balanced * balanced, axis=(1, 2)))
    reflect = (balanced * lax.rsqrt(mean_square + EPSILON)[:, None, None]).astype(jnp.bfloat16)
    rising_all = []
    for section in range(sections):
        if section + 1 < sections:
            rising_wave = up_state[section + 1]
        else:
            rising_wave = jnp.zeros_like(up_state[0])
        for inner in reversed(range(LAYERS)):
            layer_index = section * LAYERS + inner
            scattered = reflect[layer_index].astype(jnp.float32)[None, None] * sources[layer_index].astype(jnp.float32)
            rising_wave = (rising_wave.astype(jnp.float32) + scattered).astype(jnp.bfloat16)
            rising_wave = advance(rising_wave, angular_freq, slowness[layer_index], reference_slow[layer_index], tables)
        rising_all.append(rising_wave)
    return (reflect, jnp.stack(rising_all))
```

```python
import functools

import jax
import jax.numpy as jnp
import numpy as np
from jax import lax
from jax.experimental import pallas as pl
from jax.experimental.pallas import tpu as pltpu
from jax.sharding import PartitionSpec as P

TICKS = 3
EPSILON = 1e-06
F32 = jnp.float32
BF16 = jnp.bfloat16
MESH = pl.DeviceIdType.MESH
PAD = 16


def cos_sin(angle):
    turns = jnp.floor(angle * (0.5 / np.pi) + 0.5)
    half = (angle - turns * (2.0 * np.pi)) * 0.5
    sq = half * half
    s = 1.0 / 6227020800.0
    for c in (-1.0 / 39916800, 1.0 / 362880, -1.0 / 5040, 1.0 / 120, -1.0 / 6, 1.0):
        s = s * sq + c
    s = s * half
    k = 1.0 / 479001600
    for c in (-1.0 / 3628800, 1.0 / 40320, -1.0 / 720, 1.0 / 24, -0.5, 1.0):
        k = k * sq + c
    return 1.0 - 2.0 * s * s, 2.0 * s * k


def kernel(
    sizes, ang, classes, top, surface, up_in, vc, detail, cos_t, sin_t,
    refl_out, up_out,
    wmat, lmat, cur, half, shifted, back, kept, params, packed, surf, rising, far_src,
    imgs, gathered, zsend, zrecv, total0, bal,
    surf_sem, up_sem, pk_send, pk_recv, src_sem, rs_send, rs_recv, z_send, z_recv, ag_send, ag_recv,
):
    n, nd, nf, blocks, ncls = sizes
    d, f = lax.axis_index("depth"), lax.axis_index("freq")
    rows = n // nf
    step_rows = n // blocks
    w = ang[0]

    def at(shift):
        return (lax.rem(d + shift + nd, nd), f)

    def peer(k):
        return lax.rem(f + k, nf)

    def up_copy():
        return pltpu.make_async_remote_copy(
            src_ref=up_in, dst_ref=rising, send_sem=up_sem.at[0], recv_sem=up_sem.at[1],
            device_id=at(-1), device_id_type=MESH)

    def pk_copy(t):
        return pltpu.make_async_remote_copy(
            src_ref=packed.at[0], dst_ref=packed.at[t], send_sem=pk_send.at[t],
            recv_sem=pk_recv.at[t], device_id=at(-t), device_id_type=MESH)

    def src_copy():
        return pltpu.make_async_remote_copy(
            src_ref=kept.at[TICKS - 1], dst_ref=far_src, send_sem=src_sem.at[0],
            recv_sem=src_sem.at[1], device_id=at(TICKS - 1), device_id_type=MESH)

    def rs_copy(t, k):
        return pltpu.make_async_remote_copy(
            src_ref=imgs.at[t, peer(k)], dst_ref=gathered.at[t, k], send_sem=rs_send.at[t, k],
            recv_sem=rs_recv.at[t, k], device_id=(d, peer(k)), device_id_type=MESH)

    def z_copy(t):
        return pltpu.make_async_remote_copy(
            src_ref=zsend.at[t], dst_ref=zrecv.at[t], send_sem=z_send.at[t],
            recv_sem=z_recv.at[t], device_id=at(t), device_id_type=MESH)

    def ag_copy(k):
        return pltpu.make_async_remote_copy(
            src_ref=bal.at[0], dst_ref=bal.at[k], send_sem=ag_send.at[k],
            recv_sem=ag_recv.at[k], device_id=(d, peer(k)), device_id_type=MESH)

    surf_copy = pltpu.make_async_copy(
        surface.at[jnp.minimum(nd - 1 - d, TICKS - 2)],
        surf, surf_sem.at[0])

    @pl.when(d >= nd - (TICKS - 1))
    def _():
        surf_copy.start()

    barrier = pltpu.get_barrier_semaphore()
    shifts = [s for s in range(-(TICKS - 1), TICKS) if s != 0]
    for s in shifts:
        pl.semaphore_signal(barrier, inc=1, device_id=at(s), device_id_type=MESH)
    for k in range(1, nf):
        pl.semaphore_signal(barrier, inc=1, device_id=(d, peer(k)), device_id_type=MESH)

    def slow_rows(i):
        ids = vc[i : i + 1, :]
        val = jnp.zeros((1, n), F32)
        for c in range(ncls):
            val = val + jnp.where(ids == c, classes[c], 0.0)
        return val * detail[i * step_rows : (i + 1) * step_rows, :]

    acc = jnp.zeros((step_rows, n), F32)
    for i in range(blocks):
        acc = acc + slow_rows(i)
    ref_own = jnp.sum(acc, keepdims=True) * (1.0 / (n * n))
    for i in range(blocks):
        packed[0, i * step_rows : (i + 1) * step_rows, :] = (slow_rows(i) - ref_own).astype(BF16)
    hi = ref_own.astype(BF16)
    lo = (ref_own - hi.astype(F32)).astype(BF16)
    packed[0, n : n + PAD, :] = jnp.broadcast_to(hi, (PAD, n))
    packed[0, n + PAD : n + 2 * PAD, :] = jnp.broadcast_to(lo, (PAD, n))

    pl.semaphore_wait(barrier, len(shifts) + nf - 1)
    for t in range(1, TICKS):
        pk_copy(t).start()

    @pl.when(d > 0)
    def _():
        up_copy().start()

    c, s = cos_t[...], sin_t[...]
    wmat[:n, :n] = c
    wmat[n:, n:] = c
    wmat[:n, n:] = -s
    wmat[n:, :n] = s
    lmat[:n, :n] = c
    lmat[n:, n:] = c
    lmat[:n, n:] = s
    lmat[n:, :n] = -s

    chunk = 32

    def make_params(t):
        ref = packed[t, n : n + 1, 0:1].astype(F32) + packed[t, n + PAD : n + PAD + 1, 0:1].astype(F32)
        limit = (w * ref) * (w * ref)
        col = lax.broadcasted_iota(jnp.int32, (1, n), 1)
        kcol = jnp.where(col < n // 2, col, col - n).astype(F32) * (2.0 * np.pi / n)
        kcol = kcol * kcol

        def body(i, _):
            off = pl.multiple_of(i * chunk, chunk)
            row = lax.broadcasted_iota(jnp.int32, (chunk, 1), 0) + off
            krow = jnp.where(row < n // 2, row, row - n).astype(F32) * (2.0 * np.pi / n)
            q = limit - (krow * krow + kcol)
            root = jnp.sqrt(jnp.abs(q))
            decay = jnp.where(q < 0.0, jnp.exp(-root), 1.0) * (1.0 / (n * n))
            pc, ps = cos_sin(jnp.where(q > 0.0, root, 0.0))
            params[t, 0, pl.ds(off, chunk), :] = decay * pc
            params[t, 1, pl.ds(off, chunk), :] = decay * ps
            lc, ls = cos_sin(w * packed[t, pl.ds(off, chunk), :].astype(F32))
            params[t, 2, pl.ds(off, chunk), :] = lc
            params[t, 3, pl.ds(off, chunk), :] = ls
            return 0

        lax.fori_loop(0, n // chunk, body, 0)

    def load(ref, member):
        cur[:, :n] = ref[member, 0]
        cur[:, n:] = ref[member, 1]

    def reduce_tick(t):
        for k in range(1, nf):
            rs_copy(t, k).wait()
        tot = imgs[t, f].astype(F32)
        for k in range(1, nf):
            tot = tot + gathered[t, k].astype(F32)
        return tot

    def run_step(j, _):
        tick = lax.rem(j, TICKS)

        for t in range(TICKS):
            @pl.when(j == t)
            def _():
                if t > 0:
                    pk_copy(t).wait()
                make_params(t)

        for m in range(2):
            @pl.when(j == m * TICKS)
            def _():
                load(top, m)

        for t in range(1, TICKS):
            for m in range(2):
                @pl.when((j == m * TICKS + t) & (d == nd - t))
                def _():
                    if m == 0:
                        surf_copy.wait()
                    load(surf, m)

        @pl.when(j == 2 * TICKS)
        def _():
            tot2 = reduce_tick(TICKS - 1)
            zsend[TICKS - 1] = tot2.astype(BF16)
            z_copy(TICKS - 1).start()
            z_copy(1).wait()
            part = total0[...] + zrecv[1].astype(F32)
            z_copy(TICKS - 1).wait()
            part = part + zrecv[TICKS - 1].astype(F32)
            damp = part[2 * rows : 2 * rows + 1, 0:1]
            bal[0] = (part[:rows] / (part[rows : 2 * rows] + damp)).astype(BF16)
            for k in range(1, nf):
                ag_copy(k).start()
            sq = bal[0].astype(F32)
            sq = sq * sq
            for k in range(1, nf):
                ag_copy(k).wait()
                v = bal[k].astype(F32)
                sq = sq + v * v
            mean_sq = jnp.sum(sq, keepdims=True) * (1.0 / (n * n))
            scale = lax.rsqrt(mean_sq + EPSILON)
            refl_out[...] = (bal[0].astype(F32) * scale).astype(BF16)
            src_copy().wait()

            @pl.when(d < nd - 1)
            def _():
                up_copy().wait_recv()

            @pl.when(d == nd - 1)
            def _():
                rising[...] = jnp.zeros_like(rising)

            @pl.when(d > 0)
            def _():
                up_copy().wait_send()

            for k in range(nf):
                owner = lax.rem(f + nf - k, nf)
                off = pl.multiple_of(owner * rows, rows)
                r = (bal[k].astype(F32) * scale).astype(BF16).astype(F32)
                for part_i in range(2):
                    lanes = slice(part_i * n, (part_i + 1) * n)
                    cur[pl.ds(off, rows), lanes] = (
                        rising[part_i, pl.ds(off, rows), :].astype(F32)
                        + r * far_src[pl.ds(off, rows), lanes].astype(F32)
                    ).astype(BF16)

        slot = jnp.where(j == 2 * TICKS, 0, tick)

        res = jnp.dot(cur[...], wmat[...], preferred_element_type=F32)
        half[:n, :] = res[:, :n].astype(BF16)
        half[n:, :] = res[:, n:].astype(BF16)
        v = jnp.dot(lmat[...], half[...], preferred_element_type=F32)
        vr, vi = v[:n], v[n:]
        hr, hm = params[slot, 0], params[slot, 1]
        shifted[:n, :] = (vr * hr - vi * hm).astype(BF16)
        shifted[n:, :] = (vr * hm + vi * hr).astype(BF16)
        x = jnp.dot(wmat[...], shifted[...], preferred_element_type=F32)
        back[:, :n] = x[:n].astype(BF16)
        back[:, n:] = x[n:].astype(BF16)
        y = jnp.dot(back[...], lmat[...], preferred_element_type=F32)
        yr, yi = y[:, :n], y[:, n:]
        lc, ls = params[slot, 2], params[slot, 3]
        cur[:, :n] = (yr * lc - yi * ls).astype(BF16)
        cur[:, n:] = (yr * ls + yi * lc).astype(BF16)

        for t in range(TICKS):
            @pl.when(j == t)
            def _():
                kept[t] = cur[...]
                if t == TICKS - 1:
                    src_copy().start()

            @pl.when(j == TICKS + t)
            def _():
                acc_i = jnp.zeros((1, n), F32)
                for g in range(nf):
                    rs = slice(g * rows, (g + 1) * rows)
                    sr, si = kept[t, rs, :n].astype(F32), kept[t, rs, n:].astype(F32)
                    rr, ri = cur[rs, :n].astype(F32), cur[rs, n:].astype(F32)
                    ill = sr * sr + si * si
                    imgs[t, g, :rows, :] = (sr * rr + si * ri).astype(BF16)
                    imgs[t, g, rows : 2 * rows, :] = ill.astype(BF16)
                    acc_i = acc_i + jnp.sum(ill, axis=0, keepdims=True)
                mean_i = jnp.sum(acc_i, keepdims=True) * (1.0 / (n * n))
                for g in range(nf):
                    imgs[t, g, 2 * rows :, :] = jnp.broadcast_to(mean_i, (PAD, n)).astype(BF16)
                for k in range(1, nf):
                    rs_copy(t, k).start()
                if t == 1:
                    total0[...] = reduce_tick(0)
                if t == TICKS - 1:
                    zsend[1] = reduce_tick(1).astype(BF16)
                    z_copy(1).start()

        return 0

    lax.fori_loop(0, 2 * TICKS + 1, run_step, 0)
    up_out[0] = cur[:, :n]
    up_out[1] = cur[:, n:]


def per_device(fields_top, surface, up_state, angular_freq, class_slowness, velocity_class, slowness_detail):
    n = fields_top.shape[-1]
    nd, nf = lax.axis_size("depth"), lax.axis_size("freq")
    blocks = velocity_class.shape[-1]
    ncls = class_slowness.shape[0]
    rows = n // nf
    vc = jnp.repeat(velocity_class[0], n // blocks, axis=1)
    pos = np.arange(n)
    ang = (pos[:, None] * pos[None, :] % n) * (2.0 * np.pi / n)
    cos_t = jnp.asarray(np.cos(ang).astype(np.float32)).astype(BF16)
    sin_t = jnp.asarray(np.sin(ang).astype(np.float32)).astype(BF16)
    vmem = pl.BlockSpec(memory_space=pltpu.VMEM)
    smem = pl.BlockSpec(memory_space=pltpu.SMEM)
    V = pltpu.VMEM
    DMA = pltpu.SemaphoreType.DMA
    blk = 2 * rows + PAD
    refl, up = pl.pallas_call(
        functools.partial(kernel, (n, nd, nf, blocks, ncls)),
        out_shape=(
            jax.ShapeDtypeStruct((rows, n), BF16),
            jax.ShapeDtypeStruct((2, n, n), BF16),
        ),
        in_specs=[smem, smem, vmem, pl.BlockSpec(memory_space=pl.ANY), vmem, vmem, vmem, vmem, vmem],
        out_specs=(vmem, vmem),
        scratch_shapes=[
            V((2 * n, 2 * n), BF16), V((2 * n, 2 * n), BF16),
            V((n, 2 * n), BF16), V((2 * n, n), BF16), V((2 * n, n), BF16), V((n, 2 * n), BF16),
            V((TICKS, n, 2 * n), BF16), V((TICKS, 4, n, n), F32),
            V((TICKS, n + 2 * PAD, n), BF16), V((2, 2, n, n), BF16),
            V((2, n, n), BF16), V((n, 2 * n), BF16),
            V((TICKS, nf, blk, n), BF16), V((TICKS, nf, blk, n), BF16),
            V((TICKS, blk, n), BF16), V((TICKS, blk, n), BF16), V((blk, n), F32),
            V((nf, rows, n), BF16),
            DMA((1,)), DMA((2,)), DMA((TICKS,)), DMA((TICKS,)), DMA((2,)),
            DMA((TICKS, nf)), DMA((TICKS, nf)), DMA((TICKS,)), DMA((TICKS,)), DMA((nf,)), DMA((nf,)),
        ],
        compiler_params=pltpu.CompilerParams(
            collective_id=0, has_side_effects=True, vmem_limit_bytes=60 * 1024 * 1024
        ),
        name="window",
    )(
        angular_freq, class_slowness, fields_top[0, :, 0], surface[:, :, 0], up_state[0, 0], vc,
        slowness_detail[0], cos_t, sin_t,
    )
    return refl[None], up[None, None]


def solution(mesh):
    return jax.shard_map(
        per_device,
        mesh=mesh,
        in_specs=(
            P("depth", None, "freq", None, None, None),
            P(None, None, "freq", None, None, None),
            P("depth", "freq", None, None, None),
            P("freq"),
            P(),
            P("depth", None, None),
            P("depth", None, None),
        ),
        out_specs=(P("depth", "freq", None), P("depth", "freq", None, None, None)),
        check_vma=False,
    )
```

```python
import functools

import jax
import jax.numpy as jnp
import numpy as np
from jax import lax
from jax.experimental import pallas as pl
from jax.experimental.pallas import tpu as pltpu
from jax.sharding import PartitionSpec as P

TICKS = 3
EPSILON = 1e-06
F32 = jnp.float32
BF16 = jnp.bfloat16
MESH = pl.DeviceIdType.MESH
PAD = 16


def cos_sin(angle):
    turns = jnp.floor(angle * (0.5 / np.pi) + 0.5)
    half = (angle - turns * (2.0 * np.pi)) * 0.5
    sq = half * half
    s = 1.0 / 6227020800.0
    for c in (-1.0 / 39916800, 1.0 / 362880, -1.0 / 5040, 1.0 / 120, -1.0 / 6, 1.0):
        s = s * sq + c
    s = s * half
    k = 1.0 / 479001600
    for c in (-1.0 / 3628800, 1.0 / 40320, -1.0 / 720, 1.0 / 24, -0.5, 1.0):
        k = k * sq + c
    return 1.0 - 2.0 * s * s, 2.0 * s * k


def kernel(
    sizes, ang, classes, top, surface, up_in, vc, detail, cos_t, sin_t,
    refl_out, up_out,
    wmat, lmat, cur, half, shifted, back, kept, params, packed, surf, rising, far_src,
    imgs, gathered, xrecv, zsend, zrecv, total0, bal, rstate,
    surf_sem, up_sem, pk_send, pk_recv, src_sem, rs_send, rs_recv, z_sem, x_sem, ag_send, ag_recv,
):
    n, nd, nf, blocks, ncls = sizes
    d, f = lax.axis_index("depth"), lax.axis_index("freq")
    rows = n // nf
    step_rows = n // blocks
    w = ang[0]

    def at(shift):
        return (lax.rem(d + shift + nd, nd), f)

    def peer(k):
        return lax.rem(f + k, nf)

    def up_copy():
        return pltpu.make_async_remote_copy(
            src_ref=up_in, dst_ref=rising, send_sem=up_sem.at[0], recv_sem=up_sem.at[1],
            device_id=at(-1), device_id_type=MESH)

    odd = lax.rem(d, 2) == 1
    even = lax.rem(d, 2) == 0

    def pk_copy(src, dst, shift):
        return pltpu.make_async_remote_copy(
            src_ref=packed.at[src], dst_ref=packed.at[dst], send_sem=pk_send.at[src, dst],
            recv_sem=pk_recv.at[dst], device_id=at(shift), device_id_type=MESH)

    def src_copy():
        return pltpu.make_async_remote_copy(
            src_ref=kept.at[TICKS - 1], dst_ref=far_src, send_sem=src_sem.at[0],
            recv_sem=src_sem.at[1], device_id=at(TICKS - 1), device_id_type=MESH)

    def rs_copy(t, k):
        return pltpu.make_async_remote_copy(
            src_ref=imgs.at[t, peer(k)], dst_ref=gathered.at[t // 2, k],
            send_sem=rs_send.at[t // 2, k], recv_sem=rs_recv.at[t // 2, k],
            device_id=(d, peer(k)), device_id_type=MESH)

    def x_copy():
        return pltpu.make_async_remote_copy(
            src_ref=imgs.at[1], dst_ref=xrecv, send_sem=x_sem.at[0], recv_sem=x_sem.at[1],
            device_id=(d + 1 - 2 * lax.rem(d, 2), f), device_id_type=MESH)

    def z_copy():
        return pltpu.make_async_remote_copy(
            src_ref=zsend, dst_ref=zrecv, send_sem=z_sem.at[0], recv_sem=z_sem.at[1],
            device_id=at(TICKS - 1), device_id_type=MESH)

    def ag_copy(k):
        return pltpu.make_async_remote_copy(
            src_ref=bal.at[0], dst_ref=bal.at[k], send_sem=ag_send.at[k],
            recv_sem=ag_recv.at[k], device_id=(d, peer(k)), device_id_type=MESH)

    surf_copy = pltpu.make_async_copy(
        surface.at[jnp.minimum(nd - 1 - d, TICKS - 2)],
        surf, surf_sem.at[0])

    @pl.when(d >= nd - (TICKS - 1))
    def _():
        surf_copy.start()

    barrier = pltpu.get_barrier_semaphore()
    shifts = [s for s in range(-(TICKS - 1), TICKS) if s != 0]
    for s in shifts:
        pl.semaphore_signal(barrier, inc=1, device_id=at(s), device_id_type=MESH)
    for k in range(1, nf):
        pl.semaphore_signal(barrier, inc=1, device_id=(d, peer(k)), device_id_type=MESH)

    ids = vc[...]
    block_val = jnp.zeros(ids.shape, F32)
    for c in range(ncls):
        block_val = block_val + jnp.where(ids == c, classes[c], 0.0)
    col_id = lax.broadcasted_iota(jnp.int32, (1, n), 1)

    def slow_rows(i):
        val = jnp.zeros((1, n), F32)
        for b in range(blocks):
            inside = (col_id >= b * step_rows) & (col_id < (b + 1) * step_rows)
            val = jnp.where(inside, block_val[i : i + 1, b : b + 1], val)
        return val * detail[i * step_rows : (i + 1) * step_rows, :]

    acc = jnp.zeros((step_rows, n), F32)
    for i in range(blocks):
        acc = acc + slow_rows(i)
    ref_own = jnp.sum(acc, keepdims=True) * (1.0 / (n * n))
    for i in range(blocks):
        packed[0, i * step_rows : (i + 1) * step_rows, :] = (slow_rows(i) - ref_own).astype(BF16)
    hi = ref_own.astype(BF16)
    lo = (ref_own - hi.astype(F32)).astype(BF16)
    packed[0, n:, :128] = jnp.broadcast_to(hi, (PAD, 128))
    packed[0, n:, 128:] = jnp.broadcast_to(lo, (PAD, n - 128))

    pl.semaphore_wait(barrier, len(shifts) + nf - 1)
    pk_copy(0, 1, -1).start()

    @pl.when(odd)
    def _():
        pk_copy(0, 2, -2).start()

    c, s = cos_t[...], sin_t[...]
    wmat[:n, :n] = c
    wmat[n:, n:] = c
    wmat[:n, n:] = -s
    wmat[n:, :n] = s
    lmat[:n, :n] = c
    lmat[n:, n:] = c
    lmat[:n, n:] = s
    lmat[n:, :n] = -s

    chunk = 32

    def make_params(t):
        ref = packed[t, n : n + 1, 0:1].astype(F32) + packed[t, n : n + 1, 128:129].astype(F32)
        limit = (w * ref) * (w * ref)
        col = lax.broadcasted_iota(jnp.int32, (1, n), 1)
        kcol = jnp.where(col < n // 2, col, col - n).astype(F32) * (2.0 * np.pi / n)
        kcol = kcol * kcol

        def body(i, _):
            off = pl.multiple_of(i * chunk, chunk)
            row = lax.broadcasted_iota(jnp.int32, (chunk, 1), 0) + off
            krow = jnp.where(row < n // 2, row, row - n).astype(F32) * (2.0 * np.pi / n)
            q = limit - (krow * krow + kcol)
            root = jnp.sqrt(jnp.abs(q))
            decay = jnp.where(q < 0.0, jnp.exp(-root), 1.0) * (1.0 / (n * n))
            pc, ps = cos_sin(jnp.where(q > 0.0, root, 0.0))
            params[t, 0, pl.ds(off, chunk), :] = decay * pc
            params[t, 1, pl.ds(off, chunk), :] = decay * ps
            lc, ls = cos_sin(w * packed[t, pl.ds(off, chunk), :].astype(F32))
            params[t, 2, pl.ds(off, chunk), :] = lc
            params[t, 3, pl.ds(off, chunk), :] = ls
            return 0

        lax.fori_loop(0, n // chunk, body, 0)

    def load(ref, member):
        cur[:, :n] = ref[member, 0]
        cur[:, n:] = ref[member, 1]

    def reduce_tick(t):
        for k in range(1, nf):
            rs_copy(t, k).wait()
        tot = imgs[t, f].astype(F32)
        for k in range(1, nf):
            tot = tot + gathered[t // 2, k].astype(F32)
        return tot

    def start_rs(t):
        for k in range(1, nf):
            rs_copy(t, k).start()

    def add_partner(t):
        x_copy().wait()
        for g in range(nf):
            imgs[t, g] = (imgs[t, g].astype(F32) + xrecv[g].astype(F32)).astype(BF16)
        start_rs(t)

    def run_step(j, _):
        @pl.when(j == 0)
        def _():
            make_params(0)

        @pl.when(j == 2)
        def _():
            pk_copy(0, 1, -1).wait()

            @pl.when(odd)
            def _():
                pk_copy(1, 2, -1).start()

            make_params(1)

        @pl.when(j == 4)
        def _():
            @pl.when(odd)
            def _():
                pk_copy(0, 2, -2).wait()
                pk_copy(1, 2, -1).wait_send()

            @pl.when(even)
            def _():
                pk_copy(1, 2, -1).wait_recv()

            @pl.when(d > 0)
            def _():
                up_copy().start()

            make_params(2)

        @pl.when((j == 5) & odd)
        def _():
            add_partner(0)

        for m in range(2):
            @pl.when(j == m)
            def _():
                load(top, m)

        for t in range(1, TICKS):
            @pl.when(j == 2 * t)
            def _():
                cur[...] = kept[t - 1]

            @pl.when(j == 2 * t + 1)
            def _():
                cur[...] = rstate[...]

            for m in range(2):
                @pl.when((j == 2 * t + m) & (d == nd - t))
                def _():
                    if m == 0:
                        surf_copy.wait()
                    load(surf, m)

        @pl.when(j == 2 * TICKS)
        def _():
            zsend[...] = reduce_tick(2).astype(BF16)
            z_copy().start()
            total0[...] = reduce_tick(0)
            z_copy().wait()
            part = total0[...] + zrecv[...].astype(F32)
            damp = part[2 * rows : 2 * rows + 1, 0:1]
            bal[0] = (part[:rows] / (part[rows : 2 * rows] + damp)).astype(BF16)
            for k in range(1, nf):
                ag_copy(k).start()
            sq = bal[0].astype(F32)
            sq = sq * sq
            for k in range(1, nf):
                ag_copy(k).wait()
                v = bal[k].astype(F32)
                sq = sq + v * v
            mean_sq = jnp.sum(sq, keepdims=True) * (1.0 / (n * n))
            scale = lax.rsqrt(mean_sq + EPSILON)
            refl_out[...] = (bal[0].astype(F32) * scale).astype(BF16)
            src_copy().wait()

            @pl.when(d < nd - 1)
            def _():
                up_copy().wait_recv()

            @pl.when(d == nd - 1)
            def _():
                rising[...] = jnp.zeros_like(rising)

            @pl.when(d > 0)
            def _():
                up_copy().wait_send()

            for k in range(nf):
                owner = lax.rem(f + nf - k, nf)
                off = pl.multiple_of(owner * rows, rows)
                r = (bal[k].astype(F32) * scale).astype(BF16).astype(F32)
                for part_i in range(2):
                    lanes = slice(part_i * n, (part_i + 1) * n)
                    cur[pl.ds(off, rows), lanes] = (
                        rising[part_i, pl.ds(off, rows), :].astype(F32)
                        + r * far_src[pl.ds(off, rows), lanes].astype(F32)
                    ).astype(BF16)

        slot = jnp.where(j == 2 * TICKS, 0, j // 2)

        res = jnp.dot(cur[...], wmat[...], preferred_element_type=F32)
        half[:n, :] = res[:, :n].astype(BF16)
        half[n:, :] = res[:, n:].astype(BF16)
        v = jnp.dot(lmat[...], half[...], preferred_element_type=F32)
        vr, vi = v[:n], v[n:]
        hr, hm = params[slot, 0], params[slot, 1]
        shifted[:n, :] = (vr * hr - vi * hm).astype(BF16)
        shifted[n:, :] = (vr * hm + vi * hr).astype(BF16)
        x = jnp.dot(wmat[...], shifted[...], preferred_element_type=F32)
        back[:, :n] = x[:n].astype(BF16)
        back[:, n:] = x[n:].astype(BF16)
        y = jnp.dot(back[...], lmat[...], preferred_element_type=F32)
        yr, yi = y[:, :n], y[:, n:]
        lc, ls = params[slot, 2], params[slot, 3]
        cur[:, :n] = (yr * lc - yi * ls).astype(BF16)
        cur[:, n:] = (yr * ls + yi * lc).astype(BF16)

        for t in range(TICKS):
            @pl.when(j == 2 * t)
            def _():
                kept[t] = cur[...]
                if t == TICKS - 1:
                    src_copy().start()

            @pl.when(j == 2 * t + 1)
            def _():
                if t < TICKS - 1:
                    rstate[...] = cur[...]
                acc_i = jnp.zeros((1, n), F32)
                for g in range(nf):
                    rs = slice(g * rows, (g + 1) * rows)
                    sr, si = kept[t, rs, :n].astype(F32), kept[t, rs, n:].astype(F32)
                    rr, ri = cur[rs, :n].astype(F32), cur[rs, n:].astype(F32)
                    ill = sr * sr + si * si
                    imgs[t, g, :rows, :] = (sr * rr + si * ri).astype(BF16)
                    imgs[t, g, rows : 2 * rows, :] = ill.astype(BF16)
                    acc_i = acc_i + jnp.sum(ill, axis=0, keepdims=True)
                mean_i = jnp.sum(acc_i, keepdims=True) * (1.0 / (n * n))
                for g in range(nf):
                    imgs[t, g, 2 * rows :, :] = jnp.broadcast_to(mean_i, (PAD, n)).astype(BF16)
                if t == 0:
                    @pl.when(even)
                    def _():
                        start_rs(0)
                if t == 1:
                    x_copy().start()
                if t == 2:
                    @pl.when(even)
                    def _():
                        add_partner(2)

                    @pl.when(odd)
                    def _():
                        start_rs(2)

        return 0

    lax.fori_loop(0, 2 * TICKS + 1, run_step, 0)
    up_out[0] = cur[:, :n]
    up_out[1] = cur[:, n:]


def per_device(fields_top, surface, up_state, angular_freq, class_slowness, velocity_class, slowness_detail):
    n = fields_top.shape[-1]
    nd, nf = lax.axis_size("depth"), lax.axis_size("freq")
    blocks = velocity_class.shape[-1]
    ncls = class_slowness.shape[0]
    rows = n // nf
    vc = velocity_class[0]
    pos = np.arange(n)
    ang = (pos[:, None] * pos[None, :] % n) * (2.0 * np.pi / n)
    cos_t = jnp.asarray(np.cos(ang).astype(np.float32)).astype(BF16)
    sin_t = jnp.asarray(np.sin(ang).astype(np.float32)).astype(BF16)
    vmem = pl.BlockSpec(memory_space=pltpu.VMEM)
    smem = pl.BlockSpec(memory_space=pltpu.SMEM)
    V = pltpu.VMEM
    DMA = pltpu.SemaphoreType.DMA
    blk = 2 * rows + PAD
    refl, up = pl.pallas_call(
        functools.partial(kernel, (n, nd, nf, blocks, ncls)),
        out_shape=(
            jax.ShapeDtypeStruct((rows, n), BF16),
            jax.ShapeDtypeStruct((2, n, n), BF16),
        ),
        in_specs=[smem, smem, vmem, pl.BlockSpec(memory_space=pl.ANY), vmem, vmem, vmem, vmem, vmem],
        out_specs=(vmem, vmem),
        scratch_shapes=[
            V((2 * n, 2 * n), BF16), V((2 * n, 2 * n), BF16),
            V((n, 2 * n), BF16), V((2 * n, n), BF16), V((2 * n, n), BF16), V((n, 2 * n), BF16),
            V((TICKS, n, 2 * n), BF16), V((TICKS, 4, n, n), F32),
            V((TICKS, n + PAD, n), BF16), V((2, 2, n, n), BF16),
            V((2, n, n), BF16), V((n, 2 * n), BF16),
            V((TICKS, nf, blk, n), BF16), V((2, nf, blk, n), BF16), V((nf, blk, n), BF16),
            V((blk, n), BF16), V((blk, n), BF16), V((blk, n), F32),
            V((nf, rows, n), BF16), V((n, 2 * n), BF16),
            DMA((1,)), DMA((2,)), DMA((2, TICKS)), DMA((TICKS,)), DMA((2,)),
            DMA((2, nf)), DMA((2, nf)), DMA((2,)), DMA((2,)), DMA((nf,)), DMA((nf,)),
        ],
        compiler_params=pltpu.CompilerParams(
            collective_id=0, has_side_effects=True, vmem_limit_bytes=60 * 1024 * 1024
        ),
        name="window",
    )(
        angular_freq, class_slowness, fields_top[0, :, 0], surface[:, :, 0], up_state[0, 0], vc,
        slowness_detail[0], cos_t, sin_t,
    )
    return refl[None], up[None, None]


def solution(mesh):
    return jax.shard_map(
        per_device,
        mesh=mesh,
        in_specs=(
            P("depth", None, "freq", None, None, None),
            P(None, None, "freq", None, None, None),
            P("depth", "freq", None, None, None),
            P("freq"),
            P(),
            P("depth", None, None),
            P("depth", None, None),
        ),
        out_specs=(P("depth", "freq", None), P("depth", "freq", None, None, None)),
        check_vma=False,
    )
```

```python
import functools

import jax
import jax.numpy as jnp
import numpy as np
from jax import lax
from jax.experimental import pallas as pl
from jax.experimental.pallas import tpu as pltpu
from jax.sharding import PartitionSpec as P

TICKS = 3
EPSILON = 1e-06
F32 = jnp.float32
BF16 = jnp.bfloat16
MESH = pl.DeviceIdType.MESH
PAD = 16


def cos_sin(angle):
    turns = jnp.floor(angle * (0.5 / np.pi) + 0.5)
    half = (angle - turns * (2.0 * np.pi)) * 0.5
    sq = half * half
    s = 1.0 / 6227020800.0
    for c in (-1.0 / 39916800, 1.0 / 362880, -1.0 / 5040, 1.0 / 120, -1.0 / 6, 1.0):
        s = s * sq + c
    s = s * half
    k = 1.0 / 479001600
    for c in (-1.0 / 3628800, 1.0 / 40320, -1.0 / 720, 1.0 / 24, -0.5, 1.0):
        k = k * sq + c
    return 1.0 - 2.0 * s * s, 2.0 * s * k


def kernel(
    sizes, ang, classes, top, surface, up_in, vc, detail, cos_t, sin_t,
    refl_out, up_out,
    wmat, lmat, cur, half, shifted, back, kept, params, packed, surf, rising, far_src,
    imgs, gathered, xrecv, zsend, zrecv, total0, bal, rstate,
    surf_sem, up_sem, pk_send, pk_recv, src_sem, rs_send, rs_recv, z_sem, x_sem, ag_send, ag_recv,
):
    n, nd, nf, blocks, ncls = sizes
    d, f = lax.axis_index("depth"), lax.axis_index("freq")
    rows = n // nf
    step_rows = n // blocks
    w = ang[0]

    def at(shift):
        return (lax.rem(d + shift + nd, nd), f)

    def peer(k):
        return lax.rem(f + k, nf)

    def up_copy():
        return pltpu.make_async_remote_copy(
            src_ref=up_in, dst_ref=rising, send_sem=up_sem.at[0], recv_sem=up_sem.at[1],
            device_id=at(-1), device_id_type=MESH)

    odd = lax.rem(d, 2) == 1
    even = lax.rem(d, 2) == 0

    def pk_copy(src, dst, shift):
        return pltpu.make_async_remote_copy(
            src_ref=packed.at[src], dst_ref=packed.at[dst], send_sem=pk_send.at[src, dst],
            recv_sem=pk_recv.at[dst], device_id=at(shift), device_id_type=MESH)

    def src_copy():
        return pltpu.make_async_remote_copy(
            src_ref=kept.at[TICKS - 1], dst_ref=far_src, send_sem=src_sem.at[0],
            recv_sem=src_sem.at[1], device_id=at(TICKS - 1), device_id_type=MESH)

    def rs_copy(t, k):
        return pltpu.make_async_remote_copy(
            src_ref=imgs.at[t, peer(k)], dst_ref=gathered.at[t // 2, k],
            send_sem=rs_send.at[t // 2, k], recv_sem=rs_recv.at[t // 2, k],
            device_id=(d, peer(k)), device_id_type=MESH)

    def x_copy():
        return pltpu.make_async_remote_copy(
            src_ref=imgs.at[1], dst_ref=xrecv, send_sem=x_sem.at[0], recv_sem=x_sem.at[1],
            device_id=(d + 1 - 2 * lax.rem(d, 2), f), device_id_type=MESH)

    def z_copy():
        return pltpu.make_async_remote_copy(
            src_ref=zsend, dst_ref=zrecv, send_sem=z_sem.at[0], recv_sem=z_sem.at[1],
            device_id=at(TICKS - 1), device_id_type=MESH)

    def ag_copy(k):
        return pltpu.make_async_remote_copy(
            src_ref=bal.at[0], dst_ref=bal.at[k], send_sem=ag_send.at[k],
            recv_sem=ag_recv.at[k], device_id=(d, peer(k)), device_id_type=MESH)

    surf_copy = pltpu.make_async_copy(
        surface.at[jnp.minimum(nd - 1 - d, TICKS - 2)],
        surf, surf_sem.at[0])

    @pl.when(d >= nd - (TICKS - 1))
    def _():
        surf_copy.start()

    barrier = pltpu.get_barrier_semaphore()
    shifts = [s for s in range(-(TICKS - 1), TICKS) if s != 0]
    for s in shifts:
        pl.semaphore_signal(barrier, inc=1, device_id=at(s), device_id_type=MESH)
    for k in range(1, nf):
        pl.semaphore_signal(barrier, inc=1, device_id=(d, peer(k)), device_id_type=MESH)

    ids = vc[...]
    block_val = jnp.zeros(ids.shape, F32)
    for c in range(ncls):
        block_val = block_val + jnp.where(ids == c, classes[c], 0.0)
    col_id = lax.broadcasted_iota(jnp.int32, (1, n), 1)

    def slow_rows(i):
        val = jnp.zeros((1, n), F32)
        for b in range(blocks):
            inside = (col_id >= b * step_rows) & (col_id < (b + 1) * step_rows)
            val = jnp.where(inside, block_val[i : i + 1, b : b + 1], val)
        return val * detail[i * step_rows : (i + 1) * step_rows, :]

    acc = jnp.zeros((step_rows, n), F32)
    for i in range(blocks):
        acc = acc + slow_rows(i)
    ref_own = jnp.sum(acc, keepdims=True) * (1.0 / (n * n))
    for i in range(blocks):
        packed[0, i * step_rows : (i + 1) * step_rows, :] = (slow_rows(i) - ref_own).astype(BF16)
    hi = ref_own.astype(BF16)
    lo = (ref_own - hi.astype(F32)).astype(BF16)
    packed[0, n:, :128] = jnp.broadcast_to(hi, (PAD, 128))
    packed[0, n:, 128:] = jnp.broadcast_to(lo, (PAD, n - 128))

    pl.semaphore_wait(barrier, len(shifts) + nf - 1)
    pk_copy(0, 1, -1).start()

    @pl.when(odd)
    def _():
        pk_copy(0, 2, -2).start()

    c, s = cos_t[...], sin_t[...]
    wmat[:n, :n] = c
    wmat[n:, n:] = c
    wmat[:n, n:] = -s
    wmat[n:, :n] = s
    lmat[:n, :n] = c
    lmat[n:, n:] = c
    lmat[:n, n:] = s
    lmat[n:, :n] = -s

    chunk = 32

    def make_params(t):
        ref = packed[t, n : n + 1, 0:1].astype(F32) + packed[t, n : n + 1, 128:129].astype(F32)
        limit = (w * ref) * (w * ref)
        col = lax.broadcasted_iota(jnp.int32, (1, n), 1)
        kcol = jnp.where(col < n // 2, col, col - n).astype(F32) * (2.0 * np.pi / n)
        kcol = kcol * kcol

        def body(i, _):
            off = pl.multiple_of(i * chunk, chunk)
            row = lax.broadcasted_iota(jnp.int32, (chunk, 1), 0) + off
            krow = jnp.where(row < n // 2, row, row - n).astype(F32) * (2.0 * np.pi / n)
            q = limit - (krow * krow + kcol)
            root = jnp.sqrt(jnp.abs(q))
            decay = jnp.where(q < 0.0, jnp.exp(-root), 1.0) * (1.0 / (n * n))
            pc, ps = cos_sin(jnp.where(q > 0.0, root, 0.0))
            params[t, 0, pl.ds(off, chunk), :] = decay * pc
            params[t, 1, pl.ds(off, chunk), :] = decay * ps
            lc, ls = cos_sin(w * packed[t, pl.ds(off, chunk), :].astype(F32))
            params[t, 2, pl.ds(off, chunk), :] = lc
            params[t, 3, pl.ds(off, chunk), :] = ls
            return 0

        lax.fori_loop(0, n // chunk, body, 0)

    def load(ref, member):
        cur[:, :n] = ref[member, 0]
        cur[:, n:] = ref[member, 1]

    def reduce_tick(t):
        for k in range(1, nf):
            rs_copy(t, k).wait()
        tot = imgs[t, f].astype(F32)
        for k in range(1, nf):
            tot = tot + gathered[t // 2, k].astype(F32)
        return tot

    def start_rs(t):
        for k in range(1, nf):
            rs_copy(t, k).start()

    def add_partner(t):
        x_copy().wait()
        for g in range(nf):
            imgs[t, g] = (imgs[t, g].astype(F32) + xrecv[g].astype(F32)).astype(BF16)
        start_rs(t)

    def run_step(j, _):
        @pl.when(j == 0)
        def _():
            make_params(0)

        @pl.when(j == 2)
        def _():
            pk_copy(0, 1, -1).wait()

            @pl.when(odd)
            def _():
                pk_copy(1, 2, -1).start()

            make_params(1)

        @pl.when(j == 4)
        def _():
            @pl.when(odd)
            def _():
                pk_copy(0, 2, -2).wait()
                pk_copy(1, 2, -1).wait_send()

            @pl.when(even)
            def _():
                pk_copy(1, 2, -1).wait_recv()

            @pl.when(d > 0)
            def _():
                up_copy().start()

            make_params(2)

            @pl.when(odd)
            def _():
                add_partner(0)

        for m in range(2):
            @pl.when(j == m)
            def _():
                load(top, m)

        for t in range(1, TICKS):
            @pl.when(j == 2 * t)
            def _():
                cur[...] = kept[t - 1]

            @pl.when(j == 2 * t + 1)
            def _():
                cur[...] = rstate[...]

            for m in range(2):
                @pl.when((j == 2 * t + m) & (d == nd - t))
                def _():
                    if m == 0:
                        surf_copy.wait()
                    load(surf, m)

        @pl.when(j == 2 * TICKS)
        def _():
            zsend[...] = reduce_tick(2).astype(BF16)
            z_copy().start()
            total0[...] = reduce_tick(0)
            z_copy().wait()
            part = total0[...] + zrecv[...].astype(F32)
            damp = part[2 * rows : 2 * rows + 1, 0:1]
            bal[0] = (part[:rows] / (part[rows : 2 * rows] + damp)).astype(BF16)
            for k in range(1, nf):
                ag_copy(k).start()
            sq = bal[0].astype(F32)
            sq = sq * sq
            for k in range(1, nf):
                ag_copy(k).wait()
                v = bal[k].astype(F32)
                sq = sq + v * v
            mean_sq = jnp.sum(sq, keepdims=True) * (1.0 / (n * n))
            scale = lax.rsqrt(mean_sq + EPSILON)
            refl_out[...] = (bal[0].astype(F32) * scale).astype(BF16)
            src_copy().wait()

            @pl.when(d < nd - 1)
            def _():
                up_copy().wait_recv()

            @pl.when(d == nd - 1)
            def _():
                rising[...] = jnp.zeros_like(rising)

            @pl.when(d > 0)
            def _():
                up_copy().wait_send()

            for k in range(nf):
                owner = lax.rem(f + nf - k, nf)
                off = pl.multiple_of(owner * rows, rows)
                r = (bal[k].astype(F32) * scale).astype(BF16).astype(F32)
                for part_i in range(2):
                    lanes = slice(part_i * n, (part_i + 1) * n)
                    cur[pl.ds(off, rows), lanes] = (
                        rising[part_i, pl.ds(off, rows), :].astype(F32)
                        + r * far_src[pl.ds(off, rows), lanes].astype(F32)
                    ).astype(BF16)

        slot = jnp.where(j == 2 * TICKS, 0, j // 2)

        res = jnp.dot(cur[...], wmat[...], preferred_element_type=F32)
        half[:n, :] = res[:, :n].astype(BF16)
        half[n:, :] = res[:, n:].astype(BF16)
        v = jnp.dot(lmat[...], half[...], preferred_element_type=F32)
        vr, vi = v[:n], v[n:]
        hr, hm = params[slot, 0], params[slot, 1]
        shifted[:n, :] = (vr * hr - vi * hm).astype(BF16)
        shifted[n:, :] = (vr * hm + vi * hr).astype(BF16)
        x = jnp.dot(wmat[...], shifted[...], preferred_element_type=F32)
        back[:, :n] = x[:n].astype(BF16)
        back[:, n:] = x[n:].astype(BF16)
        y = jnp.dot(back[...], lmat[...], preferred_element_type=F32)
        yr, yi = y[:, :n], y[:, n:]
        lc, ls = params[slot, 2], params[slot, 3]
        cur[:, :n] = (yr * lc - yi * ls).astype(BF16)
        cur[:, n:] = (yr * ls + yi * lc).astype(BF16)

        for t in range(TICKS):
            @pl.when(j == 2 * t)
            def _():
                kept[t] = cur[...]
                if t == TICKS - 1:
                    src_copy().start()

            @pl.when(j == 2 * t + 1)
            def _():
                if t < TICKS - 1:
                    rstate[...] = cur[...]
                acc_i = jnp.zeros((1, n), F32)
                for g in range(nf):
                    rs = slice(g * rows, (g + 1) * rows)
                    sr, si = kept[t, rs, :n].astype(F32), kept[t, rs, n:].astype(F32)
                    rr, ri = cur[rs, :n].astype(F32), cur[rs, n:].astype(F32)
                    ill = sr * sr + si * si
                    imgs[t, g, :rows, :] = (sr * rr + si * ri).astype(BF16)
                    imgs[t, g, rows : 2 * rows, :] = ill.astype(BF16)
                    acc_i = acc_i + jnp.sum(ill, axis=0, keepdims=True)
                mean_i = jnp.sum(acc_i, keepdims=True) * (1.0 / (n * n))
                for g in range(nf):
                    imgs[t, g, 2 * rows :, :] = jnp.broadcast_to(mean_i, (PAD, n)).astype(BF16)
                if t == 0:
                    @pl.when(even)
                    def _():
                        start_rs(0)
                if t == 1:
                    x_copy().start()
                if t == 2:
                    @pl.when(even)
                    def _():
                        add_partner(2)

                    @pl.when(odd)
                    def _():
                        start_rs(2)

        return 0

    lax.fori_loop(0, 2 * TICKS + 1, run_step, 0)
    up_out[0] = cur[:, :n]
    up_out[1] = cur[:, n:]


def per_device(fields_top, surface, up_state, angular_freq, class_slowness, velocity_class, slowness_detail):
    n = fields_top.shape[-1]
    nd, nf = lax.axis_size("depth"), lax.axis_size("freq")
    blocks = velocity_class.shape[-1]
    ncls = class_slowness.shape[0]
    rows = n // nf
    vc = velocity_class[0]
    pos = np.arange(n)
    ang = (pos[:, None] * pos[None, :] % n) * (2.0 * np.pi / n)
    cos_t = jnp.asarray(np.cos(ang).astype(np.float32)).astype(BF16)
    sin_t = jnp.asarray(np.sin(ang).astype(np.float32)).astype(BF16)
    vmem = pl.BlockSpec(memory_space=pltpu.VMEM)
    smem = pl.BlockSpec(memory_space=pltpu.SMEM)
    V = pltpu.VMEM
    DMA = pltpu.SemaphoreType.DMA
    blk = 2 * rows + PAD
    refl, up = pl.pallas_call(
        functools.partial(kernel, (n, nd, nf, blocks, ncls)),
        out_shape=(
            jax.ShapeDtypeStruct((rows, n), BF16),
            jax.ShapeDtypeStruct((2, n, n), BF16),
        ),
        in_specs=[smem, smem, vmem, pl.BlockSpec(memory_space=pl.ANY), vmem, vmem, vmem, vmem, vmem],
        out_specs=(vmem, vmem),
        scratch_shapes=[
            V((2 * n, 2 * n), BF16), V((2 * n, 2 * n), BF16),
            V((n, 2 * n), BF16), V((2 * n, n), BF16), V((2 * n, n), BF16), V((n, 2 * n), BF16),
            V((TICKS, n, 2 * n), BF16), V((TICKS, 4, n, n), F32),
            V((TICKS, n + PAD, n), BF16), V((2, 2, n, n), BF16),
            V((2, n, n), BF16), V((n, 2 * n), BF16),
            V((TICKS, nf, blk, n), BF16), V((2, nf, blk, n), BF16), V((nf, blk, n), BF16),
            V((blk, n), BF16), V((blk, n), BF16), V((blk, n), F32),
            V((nf, rows, n), BF16), V((n, 2 * n), BF16),
            DMA((1,)), DMA((2,)), DMA((2, TICKS)), DMA((TICKS,)), DMA((2,)),
            DMA((2, nf)), DMA((2, nf)), DMA((2,)), DMA((2,)), DMA((nf,)), DMA((nf,)),
        ],
        compiler_params=pltpu.CompilerParams(
            collective_id=0, has_side_effects=True, vmem_limit_bytes=60 * 1024 * 1024
        ),
        name="window",
    )(
        angular_freq, class_slowness, fields_top[0, :, 0], surface[:, :, 0], up_state[0, 0], vc,
        slowness_detail[0], cos_t, sin_t,
    )
    return refl[None], up[None, None]


def solution(mesh):
    return jax.shard_map(
        per_device,
        mesh=mesh,
        in_specs=(
            P("depth", None, "freq", None, None, None),
            P(None, None, "freq", None, None, None),
            P("depth", "freq", None, None, None),
            P("freq"),
            P(),
            P("depth", None, None),
            P("depth", None, None),
        ),
        out_specs=(P("depth", "freq", None), P("depth", "freq", None, None, None)),
        check_vma=False,
    )
```

```python
import functools

import jax
import jax.numpy as jnp
import numpy as np
from jax import lax
from jax.experimental import pallas as pl
from jax.experimental.pallas import tpu as pltpu
from jax.sharding import PartitionSpec as P

TICKS = 3
EPSILON = 1e-06
F32 = jnp.float32
BF16 = jnp.bfloat16
MESH = pl.DeviceIdType.MESH
PAD = 16


def cos_sin(angle):
    turns = jnp.floor(angle * (0.5 / np.pi) + 0.5)
    half = (angle - turns * (2.0 * np.pi)) * 0.5
    sq = half * half
    s = 1.0 / 6227020800.0
    for c in (-1.0 / 39916800, 1.0 / 362880, -1.0 / 5040, 1.0 / 120, -1.0 / 6, 1.0):
        s = s * sq + c
    s = s * half
    k = 1.0 / 479001600
    for c in (-1.0 / 3628800, 1.0 / 40320, -1.0 / 720, 1.0 / 24, -0.5, 1.0):
        k = k * sq + c
    return 1.0 - 2.0 * s * s, 2.0 * s * k


def kernel(
    sizes, ang, classes, top, surface, up_in, vc, detail, cos_t, sin_t,
    refl_out, up_out,
    wmat, lmat, cur, half, shifted, back, kept, params, packed, surf, rising, far_src,
    imgs, gathered, xrecv, zsend, zrecv, total0, bal, rstate,
    surf_sem, up_sem, pk_send, pk_recv, src_sem, rs_send, rs_recv, z_sem, x_sem, ag_send, ag_recv,
):
    n, nd, nf, blocks, ncls = sizes
    d, f = lax.axis_index("depth"), lax.axis_index("freq")
    rows = n // nf
    step_rows = n // blocks
    w = ang[0]

    def at(shift):
        return (lax.rem(d + shift + nd, nd), f)

    def peer(k):
        return lax.rem(f + k, nf)

    def up_copy():
        return pltpu.make_async_remote_copy(
            src_ref=up_in, dst_ref=rising, send_sem=up_sem.at[0], recv_sem=up_sem.at[1],
            device_id=at(-1), device_id_type=MESH)

    odd = lax.rem(d, 2) == 1
    even = lax.rem(d, 2) == 0

    def pk_copy(src, dst, shift):
        return pltpu.make_async_remote_copy(
            src_ref=packed.at[src], dst_ref=packed.at[dst], send_sem=pk_send.at[src, dst],
            recv_sem=pk_recv.at[dst], device_id=at(shift), device_id_type=MESH)

    def src_copy():
        return pltpu.make_async_remote_copy(
            src_ref=kept.at[TICKS - 1], dst_ref=far_src, send_sem=src_sem.at[0],
            recv_sem=src_sem.at[1], device_id=at(TICKS - 1), device_id_type=MESH)

    def rs_copy(t, k):
        return pltpu.make_async_remote_copy(
            src_ref=imgs.at[t, peer(k)], dst_ref=gathered.at[t // 2, k],
            send_sem=rs_send.at[t // 2, k], recv_sem=rs_recv.at[t // 2, k],
            device_id=(d, peer(k)), device_id_type=MESH)

    def x_copy():
        return pltpu.make_async_remote_copy(
            src_ref=imgs.at[1], dst_ref=xrecv, send_sem=x_sem.at[0], recv_sem=x_sem.at[1],
            device_id=(d + 1 - 2 * lax.rem(d, 2), f), device_id_type=MESH)

    def z_copy():
        return pltpu.make_async_remote_copy(
            src_ref=zsend, dst_ref=zrecv, send_sem=z_sem.at[0], recv_sem=z_sem.at[1],
            device_id=at(TICKS - 1), device_id_type=MESH)

    def ag_copy(k):
        return pltpu.make_async_remote_copy(
            src_ref=bal.at[0], dst_ref=bal.at[k], send_sem=ag_send.at[k],
            recv_sem=ag_recv.at[k], device_id=(d, peer(k)), device_id_type=MESH)

    surf_copy = pltpu.make_async_copy(
        surface.at[jnp.minimum(nd - 1 - d, TICKS - 2)],
        surf, surf_sem.at[0])

    @pl.when(d >= nd - (TICKS - 1))
    def _():
        surf_copy.start()

    barrier = pltpu.get_barrier_semaphore()
    shifts = [s for s in range(-(TICKS - 1), TICKS) if s != 0]
    for s in shifts:
        pl.semaphore_signal(barrier, inc=1, device_id=at(s), device_id_type=MESH)
    for k in range(1, nf):
        pl.semaphore_signal(barrier, inc=1, device_id=(d, peer(k)), device_id_type=MESH)

    ids = vc[...]
    block_val = jnp.zeros(ids.shape, F32)
    for c in range(ncls):
        block_val = block_val + jnp.where(ids == c, classes[c], 0.0)
    col_id = lax.broadcasted_iota(jnp.int32, (1, n), 1)

    def slow_rows(i):
        val = jnp.zeros((1, n), F32)
        for b in range(blocks):
            inside = (col_id >= b * step_rows) & (col_id < (b + 1) * step_rows)
            val = jnp.where(inside, block_val[i : i + 1, b : b + 1], val)
        return val * detail[i * step_rows : (i + 1) * step_rows, :]

    acc = jnp.zeros((step_rows, n), F32)
    for i in range(blocks):
        acc = acc + slow_rows(i)
    ref_own = jnp.sum(acc, keepdims=True) * (1.0 / (n * n))
    for i in range(blocks):
        packed[0, i * step_rows : (i + 1) * step_rows, :] = (slow_rows(i) - ref_own).astype(BF16)
    hi = ref_own.astype(BF16)
    lo = (ref_own - hi.astype(F32)).astype(BF16)
    packed[0, n:, :128] = jnp.broadcast_to(hi, (PAD, 128))
    packed[0, n:, 128:] = jnp.broadcast_to(lo, (PAD, n - 128))

    pl.semaphore_wait(barrier, len(shifts) + nf - 1)
    pk_copy(0, 1, -1).start()

    @pl.when(odd)
    def _():
        pk_copy(0, 2, -2).start()

    c, s = cos_t[...], sin_t[...]
    wmat[:n, :n] = c
    wmat[n:, n:] = c
    wmat[:n, n:] = -s
    wmat[n:, :n] = s
    lmat[:n, :n] = c
    lmat[n:, n:] = c
    lmat[:n, n:] = s
    lmat[n:, :n] = -s

    chunk = 32

    def make_params(t):
        ref = packed[t, n : n + 1, 0:1].astype(F32) + packed[t, n : n + 1, 128:129].astype(F32)
        limit = (w * ref) * (w * ref)
        col = lax.broadcasted_iota(jnp.int32, (1, n), 1)
        kcol = jnp.where(col < n // 2, col, col - n).astype(F32) * (2.0 * np.pi / n)
        kcol = kcol * kcol

        def body(i, _):
            off = pl.multiple_of(i * chunk, chunk)
            row = lax.broadcasted_iota(jnp.int32, (chunk, 1), 0) + off
            krow = jnp.where(row < n // 2, row, row - n).astype(F32) * (2.0 * np.pi / n)
            q = limit - (krow * krow + kcol)
            root = jnp.sqrt(jnp.abs(q))
            decay = jnp.where(q < 0.0, jnp.exp(-root), 1.0) * (1.0 / (n * n))
            pc, ps = cos_sin(jnp.where(q > 0.0, root, 0.0))
            params[t, 0, pl.ds(off, chunk), :] = decay * pc
            params[t, 1, pl.ds(off, chunk), :] = decay * ps
            lc, ls = cos_sin(w * packed[t, pl.ds(off, chunk), :].astype(F32))
            params[t, 2, pl.ds(off, chunk), :] = lc
            params[t, 3, pl.ds(off, chunk), :] = ls
            return 0

        lax.fori_loop(0, n // chunk, body, 0)

    def load(ref, member):
        cur[:, :n] = ref[member, 0]
        cur[:, n:] = ref[member, 1]

    def reduce_tick(t):
        for k in range(1, nf):
            rs_copy(t, k).wait()
        tot = imgs[t, f].astype(F32)
        for k in range(1, nf):
            tot = tot + gathered[t // 2, k].astype(F32)
        return tot

    def start_rs(t):
        for k in range(1, nf):
            rs_copy(t, k).start()

    def add_partner(t):
        x_copy().wait()
        for g in range(nf):
            imgs[t, g] = (imgs[t, g].astype(F32) + xrecv[g].astype(F32)).astype(BF16)
        start_rs(t)

    def run_step(j, _):
        @pl.when(j == 0)
        def _():
            make_params(0)

        @pl.when(j == 2)
        def _():
            pk_copy(0, 1, -1).wait()

            @pl.when(odd)
            def _():
                pk_copy(1, 2, -1).start()

            make_params(1)

        @pl.when(j == 4)
        def _():
            @pl.when(odd)
            def _():
                pk_copy(0, 2, -2).wait()
                pk_copy(1, 2, -1).wait_send()

            @pl.when(even)
            def _():
                pk_copy(1, 2, -1).wait_recv()

            @pl.when(d > 0)
            def _():
                up_copy().start()

            @pl.when(odd)
            def _():
                add_partner(0)

            make_params(2)

        for m in range(2):
            @pl.when(j == m)
            def _():
                load(top, m)

        for t in range(1, TICKS):
            @pl.when(j == 2 * t)
            def _():
                cur[...] = kept[t - 1]

            @pl.when(j == 2 * t + 1)
            def _():
                cur[...] = rstate[...]

            for m in range(2):
                @pl.when((j == 2 * t + m) & (d == nd - t))
                def _():
                    if m == 0:
                        surf_copy.wait()
                    load(surf, m)

        @pl.when(j == 2 * TICKS)
        def _():
            zsend[...] = reduce_tick(2).astype(BF16)
            z_copy().start()
            total0[...] = reduce_tick(0)
            z_copy().wait()
            part = total0[...] + zrecv[...].astype(F32)
            damp = part[2 * rows : 2 * rows + 1, 0:1]
            bal[0] = (part[:rows] / (part[rows : 2 * rows] + damp)).astype(BF16)
            for k in range(1, nf):
                ag_copy(k).start()
            sq = bal[0].astype(F32)
            sq = sq * sq
            for k in range(1, nf):
                ag_copy(k).wait()
                v = bal[k].astype(F32)
                sq = sq + v * v
            mean_sq = jnp.sum(sq, keepdims=True) * (1.0 / (n * n))
            scale = lax.rsqrt(mean_sq + EPSILON)
            refl_out[...] = (bal[0].astype(F32) * scale).astype(BF16)
            src_copy().wait()

            @pl.when(d < nd - 1)
            def _():
                up_copy().wait_recv()

            @pl.when(d == nd - 1)
            def _():
                rising[...] = jnp.zeros_like(rising)

            @pl.when(d > 0)
            def _():
                up_copy().wait_send()

            for k in range(nf):
                owner = lax.rem(f + nf - k, nf)
                off = pl.multiple_of(owner * rows, rows)
                r = (bal[k].astype(F32) * scale).astype(BF16).astype(F32)
                for part_i in range(2):
                    lanes = slice(part_i * n, (part_i + 1) * n)
                    cur[pl.ds(off, rows), lanes] = (
                        rising[part_i, pl.ds(off, rows), :].astype(F32)
                        + r * far_src[pl.ds(off, rows), lanes].astype(F32)
                    ).astype(BF16)

        slot = jnp.where(j == 2 * TICKS, 0, j // 2)

        res = jnp.dot(cur[...], wmat[...], preferred_element_type=F32)
        half[:n, :] = res[:, :n].astype(BF16)
        half[n:, :] = res[:, n:].astype(BF16)
        v = jnp.dot(lmat[...], half[...], preferred_element_type=F32)
        vr, vi = v[:n], v[n:]
        hr, hm = params[slot, 0], params[slot, 1]
        shifted[:n, :] = (vr * hr - vi * hm).astype(BF16)
        shifted[n:, :] = (vr * hm + vi * hr).astype(BF16)
        x = jnp.dot(wmat[...], shifted[...], preferred_element_type=F32)
        back[:, :n] = x[:n].astype(BF16)
        back[:, n:] = x[n:].astype(BF16)
        y = jnp.dot(back[...], lmat[...], preferred_element_type=F32)
        yr, yi = y[:, :n], y[:, n:]
        lc, ls = params[slot, 2], params[slot, 3]
        cur[:, :n] = (yr * lc - yi * ls).astype(BF16)
        cur[:, n:] = (yr * ls + yi * lc).astype(BF16)

        for t in range(TICKS):
            @pl.when(j == 2 * t)
            def _():
                kept[t] = cur[...]
                if t == TICKS - 1:
                    src_copy().start()

            @pl.when(j == 2 * t + 1)
            def _():
                if t < TICKS - 1:
                    rstate[...] = cur[...]
                acc_i = jnp.zeros((1, n), F32)
                for g in range(nf):
                    rs = slice(g * rows, (g + 1) * rows)
                    sr, si = kept[t, rs, :n].astype(F32), kept[t, rs, n:].astype(F32)
                    rr, ri = cur[rs, :n].astype(F32), cur[rs, n:].astype(F32)
                    ill = sr * sr + si * si
                    imgs[t, g, :rows, :] = (sr * rr + si * ri).astype(BF16)
                    imgs[t, g, rows : 2 * rows, :] = ill.astype(BF16)
                    acc_i = acc_i + jnp.sum(ill, axis=0, keepdims=True)
                mean_i = jnp.sum(acc_i, keepdims=True) * (1.0 / (n * n))
                for g in range(nf):
                    imgs[t, g, 2 * rows :, :] = jnp.broadcast_to(mean_i, (PAD, n)).astype(BF16)
                if t == 0:
                    @pl.when(even)
                    def _():
                        start_rs(0)
                if t == 1:
                    x_copy().start()
                if t == 2:
                    @pl.when(even)
                    def _():
                        add_partner(2)

                    @pl.when(odd)
                    def _():
                        start_rs(2)

        return 0

    lax.fori_loop(0, 2 * TICKS + 1, run_step, 0)
    up_out[0] = cur[:, :n]
    up_out[1] = cur[:, n:]


def per_device(fields_top, surface, up_state, angular_freq, class_slowness, velocity_class, slowness_detail):
    n = fields_top.shape[-1]
    nd, nf = lax.axis_size("depth"), lax.axis_size("freq")
    blocks = velocity_class.shape[-1]
    ncls = class_slowness.shape[0]
    rows = n // nf
    vc = velocity_class[0]
    pos = np.arange(n)
    ang = (pos[:, None] * pos[None, :] % n) * (2.0 * np.pi / n)
    cos_t = jnp.asarray(np.cos(ang).astype(np.float32)).astype(BF16)
    sin_t = jnp.asarray(np.sin(ang).astype(np.float32)).astype(BF16)
    vmem = pl.BlockSpec(memory_space=pltpu.VMEM)
    smem = pl.BlockSpec(memory_space=pltpu.SMEM)
    V = pltpu.VMEM
    DMA = pltpu.SemaphoreType.DMA
    blk = 2 * rows + PAD
    refl, up = pl.pallas_call(
        functools.partial(kernel, (n, nd, nf, blocks, ncls)),
        out_shape=(
            jax.ShapeDtypeStruct((rows, n), BF16),
            jax.ShapeDtypeStruct((2, n, n), BF16),
        ),
        in_specs=[smem, smem, vmem, pl.BlockSpec(memory_space=pl.ANY), vmem, vmem, vmem, vmem, vmem],
        out_specs=(vmem, vmem),
        scratch_shapes=[
            V((2 * n, 2 * n), BF16), V((2 * n, 2 * n), BF16),
            V((n, 2 * n), BF16), V((2 * n, n), BF16), V((2 * n, n), BF16), V((n, 2 * n), BF16),
            V((TICKS, n, 2 * n), BF16), V((TICKS, 4, n, n), F32),
            V((TICKS, n + PAD, n), BF16), V((2, 2, n, n), BF16),
            V((2, n, n), BF16), V((n, 2 * n), BF16),
            V((TICKS, nf, blk, n), BF16), V((2, nf, blk, n), BF16), V((nf, blk, n), BF16),
            V((blk, n), BF16), V((blk, n), BF16), V((blk, n), F32),
            V((nf, rows, n), BF16), V((n, 2 * n), BF16),
            DMA((1,)), DMA((2,)), DMA((2, TICKS)), DMA((TICKS,)), DMA((2,)),
            DMA((2, nf)), DMA((2, nf)), DMA((2,)), DMA((2,)), DMA((nf,)), DMA((nf,)),
        ],
        compiler_params=pltpu.CompilerParams(
            collective_id=0, has_side_effects=True, vmem_limit_bytes=60 * 1024 * 1024
        ),
        name="window",
    )(
        angular_freq, class_slowness, fields_top[0, :, 0], surface[:, :, 0], up_state[0, 0], vc,
        slowness_detail[0], cos_t, sin_t,
    )
    return refl[None], up[None, None]


def solution(mesh):
    return jax.shard_map(
        per_device,
        mesh=mesh,
        in_specs=(
            P("depth", None, "freq", None, None, None),
            P(None, None, "freq", None, None, None),
            P("depth", "freq", None, None, None),
            P("freq"),
            P(),
            P("depth", None, None),
            P("depth", None, None),
        ),
        out_specs=(P("depth", "freq", None), P("depth", "freq", None, None, None)),
        check_vma=False,
    )
```
